128 devices in a mesh: group: 8 (over x, core), member: 16 (over z, y).
Axes of the slice: x: 4, y: 4, z: 4, core: 2. Of those that a mesh axis runs over, the one named last changes fastest.
Arguments:
- embeddings: float32 [65536, 768], P(('group', 'member'))
- cluster: int32 [65536], P(('group', 'member')), may hold values from 0 to 63, as said below
- slot: int32 [65536], P(('group', 'member')), may hold values from 0 to 1023, as said below
Outputs:
- dup_score: float32 [65536], P(('group', 'member'))
The draws below stay inside these ranges and needn't reach their ends.
Inputs may be any that keep to these rules, and one draw needn't show every extreme that they name: The 512 documents of one device name distinct slots; slot // 8 is the receiving device in group-major order; in every draw one receiving device gets all 8 of its slots filled from every device. All documents of one cluster name slots of devices of one group; in each group one of its 8 clusters holds most of the group's documents.
All inputs are finite; a program needn't handle non-finite values.
Results may differ from the reference program's by a relative error of at most 0.0012.
Values may be sent and summed in bfloat16 or wider, within the bound.
A program may use at most 128 MiB of HBM per device.

```python
import math
import jax
import jax.numpy as jnp
from jax import lax

D = 768
ROWS_DEV = 512
CLU_GROUP = 8
SUBTOPICS = 64
SLOTS_DEV = 1024
CAP = 8
ROWS = 65536
CLUSTERS = 64
N_GROUP = 8
N_MEMBER = 16


dup_families = 24


def layout(key):
    devices = N_GROUP * N_MEMBER
    space = devices * CAP
    hot = jax.random.randint(jax.random.fold_in(key, 11), (), 0, devices)
    slot_ids = jnp.arange(space, dtype=jnp.int32)

    def one_source(source):
        sub = jax.random.fold_in(jax.random.fold_in(key, 12), source)
        rank = jax.random.permutation(jax.random.fold_in(sub, 1), space).astype(jnp.int32)
        order_key = jnp.where(slot_ids // CAP == hot, slot_ids - space, rank)
        chosen = jnp.argsort(order_key, stable=True)[:ROWS_DEV]
        shuffle = jax.random.permutation(jax.random.fold_in(sub, 2), ROWS_DEV)
        return chosen[shuffle].astype(jnp.int32)
    slots = jax.vmap(one_source)(jnp.arange(devices, dtype=jnp.int32)).reshape(-1)
    owner = slots // CAP // N_MEMBER
    owners = jax.random.permutation(jax.random.fold_in(key, 13), CLUSTERS).astype(jnp.int32)
    share = jax.random.randint(jax.random.fold_in(key, 14), (ROWS,), 0, 4)
    minor = jax.random.randint(jax.random.fold_in(key, 15), (ROWS,), 1, CLU_GROUP)
    pick = jnp.where(share < 3, 0, minor)
    clusters = owners[owner * CLU_GROUP + pick].astype(jnp.int32)
    copied = jax.random.randint(jax.random.fold_in(key, 16), (ROWS,), 0, 20) < 3
    family = jax.random.randint(jax.random.fold_in(key, 17), (ROWS,), 0, dup_families)
    ident = jnp.where(copied, ROWS + clusters * dup_families + family, jnp.arange(ROWS, dtype=jnp.int32))
    return (slots, clusters, ident.astype(jnp.int32), copied)


def draw_slot(key, part):
    return layout(key)[0]


def draw_cluster(key, part):
    return layout(key)[1]


def draw_embeddings(key, part):
    slots, clusters, ident, copied = layout(key)
    base = jax.random.fold_in(key, 20)

    def direction(name):
        return jax.random.normal(jax.random.fold_in(base, name), (D,), jnp.float32)
    centre_table = jax.vmap(direction)(jnp.arange(CLUSTERS, dtype=jnp.int32))
    detail_table = jax.vmap(direction)(CLUSTERS + jnp.arange(CLUSTERS * SUBTOPICS, dtype=jnp.int32))
    proto_base = jax.random.fold_in(key, 30)

    def prototype(name):
        sub = jax.random.fold_in(proto_base, name)
        topic = jax.random.randint(jax.random.fold_in(sub, 3), (), 0, SUBTOPICS)
        weight_a = jax.random.uniform(jax.random.fold_in(sub, 1), (), jnp.float32, 0.3, 1.5)
        weight_b = jax.random.uniform(jax.random.fold_in(sub, 2), (), jnp.float32, 0.0, 1.5)
        noise = jax.random.normal(jax.random.fold_in(sub, 4), (D,), jnp.float32)
        return (weight_a, weight_b, topic, noise)
    weight_a, weight_b, topic, noise = jax.vmap(prototype)(ident)
    centre = centre_table[clusters]
    detail = detail_table[clusters * SUBTOPICS + topic]
    spread = jnp.exp(jax.random.uniform(jax.random.fold_in(key, 21), (ROWS, 1), jnp.float32, math.log(0.05), math.log(0.6)))
    jitter = jnp.where(copied[:, None], spread, jnp.float32(0.0))
    fresh = jax.random.normal(jax.random.fold_in(key, 22), (ROWS, D), jnp.float32)
    rows = weight_a[:, None] * centre + weight_b[:, None] * detail + noise + jitter * fresh
    return rows


def setup_inputs(seed: int = 0) -> dict:
    arg_keys = jax.random.split(jax.random.key(seed), 4)
    embeddings = draw_embeddings(jax.random.fold_in(arg_keys[3], 71), 0)
    cluster = draw_cluster(jax.random.fold_in(arg_keys[3], 71), 0)
    slot = draw_slot(jax.random.fold_in(arg_keys[3], 71), 0)
    return {"embeddings": embeddings, "cluster": cluster, "slot": slot}


def reference(embeddings, cluster, slot):
    devices = N_GROUP * N_MEMBER
    unit = (embeddings * lax.rsqrt(lax.optimization_barrier(jnp.sum(embeddings * embeddings, axis=1, keepdims=True)) + 1e-06)).astype(jnp.bfloat16)
    source = (jnp.arange(ROWS) // ROWS_DEV).astype(jnp.int32)
    receiver = (slot // CAP).astype(jnp.int32)
    position = (receiver * SLOTS_DEV + source * CAP + slot % CAP).astype(jnp.int32)
    arrived = jnp.zeros((devices * SLOTS_DEV, D), jnp.bfloat16).at[position].set(unit)
    labels = jnp.full((devices * SLOTS_DEV,), -1, jnp.int32).at[position].set(cluster)
    group_rows = arrived.reshape(N_GROUP, N_MEMBER * SLOTS_DEV, D)
    group_labels = labels.reshape(N_GROUP, N_MEMBER * SLOTS_DEV)
    index_all = jnp.arange(N_MEMBER * SLOTS_DEV, dtype=jnp.int32)

    def one_group(pair):
        rows, clus = pair

        def one_block(block):
            start = (block * SLOTS_DEV).astype(jnp.int32)
            queries = lax.dynamic_slice_in_dim(rows, start, SLOTS_DEV, 0)
            qclu = lax.dynamic_slice_in_dim(clus, start, SLOTS_DEV, 0)
            qpos = start + jnp.arange(SLOTS_DEV, dtype=jnp.int32)
            cosine = jnp.dot(queries, rows.T, preferred_element_type=jnp.float32)
            same = (qclu[:, None] == clus[None, :]) & (clus[None, :] >= 0) & (qpos[:, None] != index_all[None, :])
            terms = jnp.where(same, jnp.exp(20.0 * (cosine - 1.0)), jnp.float32(0.0))
            return jnp.log(1.0 + lax.optimization_barrier(jnp.sum(terms, axis=1)))
        return lax.map(one_block, jnp.arange(N_MEMBER, dtype=jnp.int32)).reshape(-1)
    scores = lax.map(one_group, (group_rows, group_labels)).reshape(-1)
    return scores[position]
```

```python
import functools
import math

import jax
import jax.numpy as jnp
from jax import lax
from jax.experimental import pallas as pl
from jax.experimental.pallas import tpu as pltpu
from jax.sharding import PartitionSpec as P

D = 768
CAPB = 96
DOCS = CAPB - 1
NQ = 8
BLK = NQ * CAPB
ND = 6
FLAG_LANE = 127
SCALE = 20.0 * math.log2(math.e)
MESH = pl.DeviceIdType.MESH
HELD = ((0, 0), (1, 0), (3, 0), (2, 0), (0, 1), (0, 2))
PAIRS = (
    (0, 0, False),
    (0, 1, True),
    (0, 3, False),
    (0, 4, True),
    (1, 4, True),
    (2, 4, True),
    (3, 4, True),
    (0, 5, False),
    (1, 5, True),
    (3, 5, False),
)
ORDER = (0, 1, 2, 3, 6, 7, 4, 5)


def pack_kernel(emb_ref, slot_ref, clu_ref, send_ref, meta_ref):
    rows = emb_ref.shape[0]
    slot = slot_ref[...]
    group = slot // 128
    ids = lax.broadcasted_iota(jnp.int32, (8, rows), 0)
    member = (ids == group).astype(jnp.float32)
    upper = lax.broadcasted_iota(jnp.int32, (rows, rows), 0) < lax.broadcasted_iota(
        jnp.int32, (rows, rows), 1
    )
    before = jnp.dot(
        member.astype(jnp.bfloat16),
        upper.astype(jnp.float32).astype(jnp.bfloat16),
        preferred_element_type=jnp.float32,
    )
    rank = jnp.sum(member * before, axis=0, keepdims=True).astype(jnp.int32)
    fits = rank < DOCS
    overflow = jnp.max(jnp.where(fits, 0.0, 1.0))
    place = jnp.where(fits, group * CAPB + rank, -1)
    meta_ref[0:1, :] = group
    meta_ref[1:2, :] = rank

    values = emb_ref[...]
    squares = jnp.sum(values * values, axis=1, keepdims=True)
    unit = (values * lax.rsqrt(squares + 1e-06)).astype(jnp.bfloat16)

    lane = lax.broadcasted_iota(jnp.int32, (128, rows), 0)
    at_rank = ((lane == rank) & fits).astype(jnp.float32).astype(jnp.bfloat16)
    label = (member * (clu_ref[...] + 1).astype(jnp.float32)).astype(jnp.bfloat16)
    labels = lax.dot_general(
        label, at_rank, (((1,), (1,)), ((), ())), preferred_element_type=jnp.float32
    )
    lanes = lax.broadcasted_iota(jnp.int32, (8, 128), 1)
    labels = jnp.where(lanes == FLAG_LANE, overflow, labels)
    row = lax.broadcasted_iota(jnp.int32, (CAPB, rows), 0)
    last = lax.broadcasted_iota(jnp.int32, (CAPB, 128), 0) == DOCS
    for g in range(8):
        chosen = (row + g * CAPB == place).astype(jnp.float32).astype(jnp.bfloat16)
        packed = jnp.dot(chosen, unit, preferred_element_type=jnp.float32)
        head = jnp.where(last, labels[g : g + 1, :], packed[:, :128])
        send_ref[g, :, :128] = head.astype(jnp.bfloat16)
        send_ref[g, :, 128:] = packed[:, 128:].astype(jnp.bfloat16)


def pack(embeddings, slot, cluster):
    rows = embeddings.shape[0]
    return pl.pallas_call(
        pack_kernel,
        out_shape=(
            jax.ShapeDtypeStruct((8, CAPB, D), jnp.bfloat16),
            jax.ShapeDtypeStruct((2, rows), jnp.int32),
        ),
        in_specs=[pl.BlockSpec(memory_space=pltpu.VMEM)] * 3,
        out_specs=(pl.BlockSpec(memory_space=pltpu.VMEM),) * 2,
        compiler_params=pltpu.CompilerParams(vmem_limit_bytes=24 << 20),
        name="pack",
    )(embeddings, slot.reshape(1, rows), cluster.reshape(1, rows))


def score_kernel(
    send_ref,
    got_ref,
    blk,
    relay,
    lrow,
    lcol,
    rsum,
    csum,
    ret,
    own_sem,
    arr_sem,
    out_sem,
    rel_in,
    rel_out,
    p1_out,
    ret_in,
    ret_out,
):
    gi = lax.axis_index("group")
    mi = lax.axis_index("member")
    x, c = gi // 2, gi % 2
    z, y = mi // 4, mi % 4

    def line_coord(t):
        return x * (1 - t) + z * t

    def line_dev(t, off, core):
        return (((x + (1 - t) * off) % 4) * 2 + core, ((z + t * off) % 4) * 4 + y)

    def plane_dev(a, b):
        px = (x + c * a) % 4
        pz = (z + (1 - c) * a) % 4
        py = (y + b * (1 + 2 * c)) % 4
        return (px * 2 + c, pz * 4 + py)

    def remote(src, dst, send_sem, recv_sem, dev):
        return pltpu.make_async_remote_copy(
            src_ref=src,
            dst_ref=dst,
            send_sem=send_sem,
            recv_sem=recv_sem,
            device_id=dev,
            device_id_type=MESH,
        )

    def chunk(m, q):
        return blk.at[m, pl.ds(q * CAPB, CAPB), :]

    own = pltpu.make_async_copy(send_ref.at[2 * line_coord(c) + c], chunk(0, 0), own_sem)
    own.start()

    barrier = pltpu.get_barrier_semaphore()
    partners = [
        (x * 2 + 1 - c, mi),
        line_dev(c, 1, c),
        line_dev(c, 3, c),
        line_dev(1 - c, 1, 1 - c),
        line_dev(1 - c, 3, 1 - c),
        line_dev(c, 1, 1 - c),
        line_dev(c, 3, 1 - c),
        plane_dev(1, 0),
        plane_dev(3, 0),
        plane_dev(0, 1),
        plane_dev(0, 3),
    ]
    for dev in partners:
        pl.semaphore_signal(barrier, inc=1, device_id=dev, device_id_type=MESH)
    pl.semaphore_wait(barrier, len(partners))

    sent = []

    def start(copy):
        copy.start()
        sent.append(copy)

    for tau in (1, 0):
        t = c if tau == 0 else 1 - c
        at = line_coord(t)
        step = 1 if tau == 0 else 3
        if tau == 1:
            start(
                remote(
                    send_ref.at[2 * at + t], chunk(0, 1), p1_out.at[0], arr_sem.at[1],
                    (x * 2 + t, mi),
                )
            )
        start(
            remote(
                send_ref.at[2 * ((at + 2) % 4) + t], relay.at[tau], p1_out.at[1 + tau],
                rel_in.at[tau], line_dev(t, step, c),
            )
        )
    for off, q in ((1, 6), (3, 2)):
        for tau in (0, 1):
            t = c if tau == 0 else 1 - c
            at = line_coord(t)
            start(
                remote(
                    send_ref.at[2 * ((at + off) % 4) + t], chunk(0, q + tau),
                    p1_out.at[3 + tau + (0 if off == 1 else 2)], arr_sem.at[q + tau],
                    line_dev(t, off, t),
                )
            )

    def arrived(m, q):
        pltpu.make_async_copy(chunk(m, q), chunk(m, q), arr_sem.at[m * NQ + q]).wait()

    def pass_on(m, src, q, dev):
        start(
            remote(
                chunk(src, q), chunk(m, q), out_sem.at[(m - 1) * NQ + q],
                arr_sem.at[m * NQ + q], dev,
            )
        )

    for k in range(NQ + 1):
        if k == 2:
            for tau in (0, 1):
                t = c if tau == 0 else 1 - c
                pltpu.make_async_copy(relay.at[tau], relay.at[tau], rel_in.at[tau]).wait()
                start(
                    remote(
                        relay.at[tau], chunk(0, 4 + tau), rel_out.at[tau],
                        arr_sem.at[4 + tau], line_dev(t, 1 if tau == 0 else 3, t),
                    )
                )
        if k < NQ:
            q = ORDER[k]
            if q == 0:
                own.wait()
            else:
                arrived(0, q)
            pass_on(4, 0, q, plane_dev(0, 1))
            pass_on(1, 0, q, plane_dev(1, 0))
            pass_on(2, 0, q, plane_dev(3, 0))
        if k >= 1:
            q = ORDER[k - 1]
            arrived(4, q)
            pass_on(5, 4, q, plane_dev(0, 1))
            arrived(1, q)
            if k % 2 == 0:
                pass_on(3, 1, q, plane_dev(1, 0))
            arrived(2, q)
            if k % 2 == 1:
                pass_on(3, 2, q, plane_dev(3, 0))
    for k in range(NQ):
        arrived(3, ORDER[k])
        arrived(5, ORDER[k])

    lanes = lax.broadcasted_iota(jnp.int32, (1, 128), 1)
    overflow = jnp.zeros((1, 128), jnp.float32)
    for m in range(ND):
        rows = []
        for q in range(NQ):
            tail = blk[m, pl.ds(q * CAPB + CAPB - 16, 16), 0:128].astype(jnp.float32)
            rows.append(tail[15:16, :])
        labels = jnp.concatenate(rows, axis=0)
        overflow = jnp.maximum(overflow, jnp.max(labels, axis=0, keepdims=True))
        labels = jnp.where(lanes < DOCS, labels, 0.0)
        wide = jnp.zeros((8, BLK), jnp.float32)
        for q in range(NQ):
            piece = jnp.concatenate(
                [jnp.broadcast_to(labels[q : q + 1, :], (8, 128)), jnp.zeros((8, BLK - 128), jnp.float32)],
                axis=1,
            )
            wide = wide + (pltpu.roll(piece, q * CAPB, axis=1) if q else piece)
        lrow[m] = wide
        full = jnp.concatenate([labels, jnp.zeros((120, 128), jnp.float32)], axis=0)
        turned = jnp.transpose(full)
        for q in range(NQ):
            column = jnp.broadcast_to(turned[0:CAPB, q : q + 1], (CAPB, 128))
            lcol[m, pl.ds(q * CAPB, CAPB), :] = jnp.where(column == 0.0, -1.0, column)

    rsum[...] = jnp.zeros_like(rsum)
    csum[...] = jnp.zeros_like(csum)
    tile = 256
    for i, j, both in PAIRS:

        @pl.loop(0, BLK // tile)
        def _(r):
            at = pl.multiple_of(r * tile, tile)
            cosine = lax.dot_general(
                blk[i, pl.ds(at, tile), :],
                blk[j],
                (((1,), (1,)), ((), ())),
                preferred_element_type=jnp.float32,
            )
            column = lcol[i, pl.ds(at, tile), :]
            total = jnp.zeros((tile, 128), jnp.float32)
            for n in range(BLK // 128):
                part = cosine[:, n * 128 : (n + 1) * 128]
                same = column == lrow[j, 0:1, n * 128 : (n + 1) * 128]
                if i == j:
                    here = at + lax.broadcasted_iota(jnp.int32, (tile, 128), 0)
                    there = n * 128 + lax.broadcasted_iota(jnp.int32, (tile, 128), 1)
                    same = same & (here != there)
                term = jnp.where(same, jnp.exp2(part * SCALE - SCALE), 0.0)
                total = total + term
                if both:
                    csum[j, :, n * 128 : (n + 1) * 128] += jnp.sum(
                        term.reshape(tile // 8, 8, 128), axis=0
                    )
            rsum[i, pl.ds(at, tile), :] += total

    flag = jnp.max(jnp.where(lanes == FLAG_LANE, overflow, 0.0))
    for m in range(ND):
        line = jnp.sum(csum[m], axis=0, keepdims=True)
        if m < 4:
            line = line + jnp.sum(jnp.transpose(rsum[m]), axis=0, keepdims=True)
        line = jnp.broadcast_to(line, (8, BLK))
        for q in range(NQ):
            piece = (pltpu.roll(line, BLK - q * CAPB, axis=1) if q else line)[0:1, 0:128]
            ret[m, q] = jnp.where(lanes == FLAG_LANE, flag, piece)
    group = 2 * line_coord(c) + c
    for m in range(ND):
        a, b = HELD[m]
        for q in range(NQ):
            if m == 0 and q == 0:
                pltpu.make_async_copy(ret.at[0, 0], got_ref.at[0, group], ret_in).start()
                continue
            dl, cs = q // 2, q % 2
            core = c if cs == 0 else 1 - c
            px = (x + c * (4 - a) + (1 - c) * dl) % 4
            pz = (z + (1 - c) * (4 - a) + c * dl) % 4
            py = (y + (4 - b) * (1 + 2 * c)) % 4
            remote(
                ret.at[m, q], got_ref.at[m, group], ret_out, ret_in, (px * 2 + core, pz * 4 + py)
            ).start()
    pltpu.make_async_copy(got_ref, got_ref, ret_in).wait()
    for copy in sent:
        copy.wait_send()
    most = ret.at[0, pl.ds(1, NQ - 1)]
    pltpu.make_async_copy(most, most, ret_out).wait()
    rest = ret.at[pl.ds(1, ND - 1)]
    pltpu.make_async_copy(rest, rest, ret_out).wait()


def partial_sums(send):
    dma = pltpu.SemaphoreType.DMA
    return pl.pallas_call(
        score_kernel,
        out_shape=jax.ShapeDtypeStruct((ND, 8, 1, 128), jnp.float32),
        in_specs=[pl.BlockSpec(memory_space=pltpu.VMEM)],
        out_specs=pl.BlockSpec(memory_space=pltpu.VMEM),
        scratch_shapes=[
            pltpu.VMEM((ND, BLK, D), jnp.bfloat16),
            pltpu.VMEM((2, CAPB, D), jnp.bfloat16),
            pltpu.VMEM((ND, 8, BLK), jnp.float32),
            pltpu.VMEM((ND, BLK, 128), jnp.float32),
            pltpu.VMEM((4, BLK, 128), jnp.float32),
            pltpu.VMEM((ND, 8, BLK), jnp.float32),
            pltpu.VMEM((ND, NQ, 1, 128), jnp.float32),
            dma(()),
            dma((ND * NQ,)),
            dma(((ND - 1) * NQ,)),
            dma((2,)),
            dma((2,)),
            dma((7,)),
            dma(()),
            dma(()),
        ],
        compiler_params=pltpu.CompilerParams(
            collective_id=0, has_side_effects=True, vmem_limit_bytes=48 << 20
        ),
        name="scores",
    )(send)


def pick_kernel(got_ref, meta_ref, out_ref, flag_ref):
    total = got_ref[0, :, 0, :]
    for m in range(1, ND):
        total = total + got_ref[m, :, 0, :]
    lanes = lax.broadcasted_iota(jnp.int32, (8, 128), 1)
    flag_ref[...] = jnp.max(jnp.where(lanes == FLAG_LANE, total, 0.0), keepdims=True)
    scores = jnp.log(1.0 + total)
    ids = lax.broadcasted_iota(jnp.int32, (8, 128), 0)
    for n in range(out_ref.shape[1] // 128):
        group = meta_ref[0:1, n * 128 : (n + 1) * 128]
        rank = jnp.broadcast_to(meta_ref[1:2, n * 128 : (n + 1) * 128], (8, 128))
        values = jnp.take_along_axis(scores, jnp.minimum(rank, 127), axis=1)
        out_ref[:, n * 128 : (n + 1) * 128] = jnp.sum(
            jnp.where(ids == group, values, 0.0), axis=0, keepdims=True
        )


def pick(got, meta):
    rows = meta.shape[1]
    return pl.pallas_call(
        pick_kernel,
        out_shape=(
            jax.ShapeDtypeStruct((1, rows), jnp.float32),
            jax.ShapeDtypeStruct((1, 1), jnp.float32),
        ),
        in_specs=[pl.BlockSpec(memory_space=pltpu.VMEM)] * 2,
        out_specs=(pl.BlockSpec(memory_space=pltpu.VMEM),) * 2,
        name="pick",
    )(got, meta)


def general(embeddings, cluster, slot):
    rows, width = embeddings.shape
    slots_dev = 2 * rows
    unit = (
        embeddings * lax.rsqrt(jnp.sum(embeddings * embeddings, axis=1, keepdims=True) + 1e-06)
    ).astype(jnp.bfloat16)
    both = ("group", "member")
    send_rows = jnp.zeros((slots_dev, width), jnp.bfloat16).at[slot].set(unit)
    send_labels = jnp.full((slots_dev,), -1, jnp.int32).at[slot].set(cluster)
    got_rows = lax.all_to_all(send_rows, both, split_axis=0, concat_axis=0, tiled=True)
    got_labels = lax.all_to_all(send_labels, both, split_axis=0, concat_axis=0, tiled=True)
    members = lax.axis_size("member")
    ring = [(i, (i + 1) % members) for i in range(members)]
    index = jnp.arange(slots_dev, dtype=jnp.int32)

    def step(turn, state):
        keys, labels, totals = state
        cosine = jnp.einsum("qd,kd->qk", got_rows, keys, preferred_element_type=jnp.float32)
        same = (got_labels[:, None] == labels[None, :]) & (labels[None, :] >= 0)
        same = same & ((index[:, None] != index[None, :]) | (turn > 0))
        terms = jnp.where(same, jnp.exp(20.0 * (cosine - 1.0)), jnp.float32(0.0))
        return (
            lax.ppermute(keys, "member", ring),
            lax.ppermute(labels, "member", ring),
            totals + jnp.sum(terms, axis=1),
        )

    zero = jnp.zeros((slots_dev,), jnp.float32)
    totals = lax.fori_loop(0, members, step, (got_rows, got_labels, zero))[2]
    scores = jnp.log(1.0 + totals)
    back = lax.all_to_all(scores, both, split_axis=0, concat_axis=0, tiled=True)
    return back[slot]


def body(embeddings, cluster, slot):
    send, meta = pack(embeddings, slot, cluster)
    got = partial_sums(send)
    out, flag = pick(got, meta)
    return lax.cond(
        flag[0, 0] > 0.0,
        lambda: general(embeddings, cluster, slot),
        lambda: out.reshape(-1),
    )


def solution(mesh):
    spec = P(("group", "member"))
    in_specs = (P(("group", "member"), None), spec, spec)
    return jax.shard_map(body, mesh=mesh, in_specs=in_specs, out_specs=spec, check_vma=False)
```

```python
import functools
import math

import jax
import jax.numpy as jnp
from jax import lax
from jax.experimental import pallas as pl
from jax.experimental.pallas import tpu as pltpu
from jax.sharding import PartitionSpec as P

D = 768
CAPB = 96
DOCS = CAPB - 1
NQ = 8
BLK = NQ * CAPB
ND = 6
HALF = BLK // 2
TILE = 256
FLAG_LANE = 127
SCALE = 20.0 * math.log2(math.e)
MESH = pl.DeviceIdType.MESH
HELD = ((0, 0), (1, 0), (3, 0), (2, 0), (0, 1), (0, 2))

def turn(c, q):
    return (c if q % 2 == 0 else 1 - c), (4 - q // 2) % 4


def plan():
    steps = [("route", q) for q in (1, 6, 7, 2, 3, 4, 5)]

    def got(m, *chunks):
        steps.extend(("wait", m, q) for q in chunks)

    def spread(q):
        if q:
            got(0, q)
        steps.extend(("pass", m, 0, q) for m in (4, 1, 2))

    def pass5(*chunks):
        for q in chunks:
            got(4, q)
            steps.append(("pass", 5, 4, q))

    def pass3(*chunks):
        for q in chunks:
            got(1, q)
            got(2, q)
            steps.append(("pass", 3, 1 + q % 2, q))

    def names(m, *halves):
        steps.extend(("names", m, h) for h in halves)

    def product(i, rows, j, cols, both):
        steps.append(("product", i, rows, j, cols, both))

    whole, first, second = (0, BLK), (0, HALF), (HALF, HALF)
    spread(0)
    spread(1)
    pass5(0)
    for q in (2, 3, 6, 7, 4, 5):
        spread(q)
    pass5(1, 2, 3)
    names(0, 0, 1)
    product(0, whole, 0, whole, False)
    pass3(0, 1, 2, 3)
    names(4, 0)
    names(1, 0)
    names(2, 0)
    product(0, whole, 4, first, True)
    product(0, whole, 1, first, True)
    pass5(6, 7)
    product(1, first, 4, first, True)
    product(2, first, 4, first, True)
    pass3(6, 7)
    pass5(4, 5)
    names(4, 1)
    product(0, whole, 4, second, True)
    pass3(4, 5)
    names(1, 1)
    names(2, 1)
    product(0, whole, 1, second, True)
    for m in (1, 2):
        product(m, second, 4, first, True)
        product(m, whole, 4, second, True)
    got(5, 0, 1, 2, 3)
    names(5, 0)
    product(0, whole, 5, first, False)
    product(1, whole, 5, first, True)
    got(3, 0, 1, 2, 3)
    names(3, 0)
    product(0, whole, 3, first, False)
    product(3, first, 4, whole, True)
    product(3, first, 5, first, False)
    got(3, 6, 7, 4, 5)
    names(3, 1)
    product(0, whole, 3, second, False)
    product(3, second, 4, whole, True)
    product(3, second, 5, first, False)
    got(5, 6, 7, 4, 5)
    names(5, 1)
    product(0, whole, 5, second, False)
    product(1, whole, 5, second, True)
    product(3, whole, 5, second, False)
    return steps


def score_kernel(
    emb_ref,
    slot_ref,
    clu_ref,
    out_ref,
    flag_ref,
    send,
    blk,
    lrow,
    lcol,
    rsum,
    csum,
    ret,
    got,
    arr_sem,
    out_sem,
    p1_out,
    ret_in,
    ret_out,
):
    gi = lax.axis_index("group")
    mi = lax.axis_index("member")
    x, c = gi // 2, gi % 2
    z, y = mi // 4, mi % 4

    def line_coord(t):
        return x * (1 - t) + z * t

    def line_dev(t, off, core):
        return (((x + (1 - t) * off) % 4) * 2 + core, ((z + t * off) % 4) * 4 + y)

    def plane_dev(a, b):
        px = (x + c * a) % 4
        pz = (z + (1 - c) * a) % 4
        py = (y + b * (1 + 2 * c)) % 4
        return (px * 2 + c, pz * 4 + py)

    def remote(src, dst, send_sem, recv_sem, dev):
        return pltpu.make_async_remote_copy(
            src_ref=src,
            dst_ref=dst,
            send_sem=send_sem,
            recv_sem=recv_sem,
            device_id=dev,
            device_id_type=MESH,
        )

    def chunk(m, q):
        return blk.at[m, pl.ds(q * CAPB, CAPB), :]

    barrier = pltpu.get_barrier_semaphore()
    partners = [(x * 2 + 1 - c, mi)]
    for off in (1, 2, 3):
        partners += [line_dev(c, off, c), line_dev(1 - c, off, 1 - c), line_dev(c, off, 1 - c)]
    partners += [plane_dev(1, 0), plane_dev(3, 0), plane_dev(0, 1), plane_dev(0, 3)]
    for dev in partners:
        pl.semaphore_signal(barrier, inc=1, device_id=dev, device_id_type=MESH)

    docs = emb_ref.shape[0]
    group = slot_ref[...] // 128
    ids = lax.broadcasted_iota(jnp.int32, (8, docs), 0)
    member = (ids == group).astype(jnp.float32)
    upper = lax.broadcasted_iota(jnp.int32, (docs, docs), 0) < lax.broadcasted_iota(
        jnp.int32, (docs, docs), 1
    )
    before = jnp.dot(
        member.astype(jnp.bfloat16),
        upper.astype(jnp.float32).astype(jnp.bfloat16),
        preferred_element_type=jnp.float32,
    )
    rank = jnp.sum(member * before, axis=0, keepdims=True).astype(jnp.int32)
    fits = rank < DOCS
    place = jnp.where(fits, group * CAPB + rank, -1)

    lane = lax.broadcasted_iota(jnp.int32, (128, docs), 0)
    at_rank = ((lane == rank) & fits).astype(jnp.float32).astype(jnp.bfloat16)
    label = (member * (clu_ref[...] + 1).astype(jnp.float32)).astype(jnp.bfloat16)
    labels = lax.dot_general(
        label, at_rank, (((1,), (1,)), ((), ())), preferred_element_type=jnp.float32
    )
    tile_lane = lax.broadcasted_iota(jnp.int32, (8, 128), 1)
    tile_row = lax.broadcasted_iota(jnp.int32, (8, 128), 0)
    labels = jnp.where(tile_lane == FLAG_LANE, jnp.max(jnp.where(fits, 0.0, 1.0)), labels)

    values = emb_ref[...]
    squares = jnp.sum(values * values, axis=1, keepdims=True)
    unit = (values * lax.rsqrt(squares + 1e-06)).astype(jnp.bfloat16)

    row = lax.broadcasted_iota(jnp.int32, (CAPB, docs), 0)
    last = lax.broadcasted_iota(jnp.int32, (CAPB, 128), 0) == DOCS

    def pack(chunks):
        owners = []
        for q in chunks:
            t, off = turn(c, q)
            owners.append(2 * ((line_coord(t) + off) % 4) + t)
        chosen = jnp.concatenate(
            [(row + g * CAPB == place).astype(jnp.float32) for g in owners], axis=0
        ).astype(jnp.bfloat16)
        packed = jnp.dot(chosen, unit, preferred_element_type=jnp.float32)
        for k, (q, g) in enumerate(zip(chunks, owners)):
            part = packed[k * CAPB : (k + 1) * CAPB]
            tail = jnp.sum(jnp.where(tile_row == g, labels, 0.0), axis=0, keepdims=True)
            part = jnp.concatenate([jnp.where(last, tail, part[:, :128]), part[:, 128:]], axis=1)
            if q:
                send[q] = part.astype(jnp.bfloat16)
            else:
                blk[0, 0:CAPB, :] = part.astype(jnp.bfloat16)

    pack((6, 7, 2, 3))
    pack((4, 5, 1, 0))
    rsum[...] = jnp.zeros_like(rsum)
    csum[...] = jnp.zeros_like(csum)
    pl.semaphore_wait(barrier, len(partners))

    sent = []

    def start(copy):
        copy.start()
        sent.append(copy)

    lanes = lax.broadcasted_iota(jnp.int32, (1, 128), 1)
    overflow = jnp.zeros((1, 128), jnp.float32)
    hops = {1: plane_dev(1, 0), 2: plane_dev(3, 0), 4: plane_dev(0, 1), 5: plane_dev(0, 1)}

    for step in plan():
        if step[0] == "route":
            q = step[1]
            t, off = turn(c, q)
            start(remote(send.at[q], chunk(0, q), p1_out.at[q], arr_sem.at[q], line_dev(t, off, t)))
        elif step[0] == "pass":
            _, m, src, q = step
            start(
                remote(
                    chunk(src, q), chunk(m, q), out_sem.at[(m - 1) * NQ + q],
                    arr_sem.at[m * NQ + q], hops[src if m == 3 else m],
                )
            )
        elif step[0] == "wait":
            _, m, q = step
            pltpu.make_async_copy(chunk(m, q), chunk(m, q), arr_sem.at[m * NQ + q]).wait()
        elif step[0] == "names":
            _, m, h = step
            rows = []
            for q in range(4 * h, 4 * h + 4):
                tail = blk[m, pl.ds(q * CAPB + CAPB - 16, 16), 0:128].astype(jnp.float32)
                rows.append(tail[15:16, :])
            found = jnp.concatenate(rows + [jnp.zeros((4, 128), jnp.float32)], axis=0)
            overflow = jnp.maximum(overflow, jnp.max(found, axis=0, keepdims=True))
            found = jnp.where(lanes < DOCS, found, 0.0)
            wide = jnp.zeros((8, HALF), jnp.float32)
            for k in range(4):
                piece = jnp.concatenate(
                    [
                        jnp.broadcast_to(found[k : k + 1, :], (8, 128)),
                        jnp.zeros((8, HALF - 128), jnp.float32),
                    ],
                    axis=1,
                )
                wide = wide + (pltpu.roll(piece, k * CAPB, axis=1) if k else piece)
            lrow[m, :, h * HALF : (h + 1) * HALF] = wide
            turned = jnp.transpose(
                jnp.concatenate([found, jnp.zeros((120, 128), jnp.float32)], axis=0)
            )
            for k in range(4):
                column = jnp.broadcast_to(turned[0:CAPB, k : k + 1], (CAPB, 128))
                lcol[m, pl.ds(h * HALF + k * CAPB, CAPB), :] = jnp.where(
                    column == 0.0, -1.0, column
                )
        else:
            _, i, (r0, nr), j, (c0, nc), both = step
            tile = TILE if nr % TILE == 0 else nr
            for at in range(r0, r0 + nr, tile):
                cosine = lax.dot_general(
                    blk[i, pl.ds(at, tile), :],
                    blk[j, pl.ds(c0, nc), :],
                    (((1,), (1,)), ((), ())),
                    preferred_element_type=jnp.float32,
                )
                column = lcol[i, pl.ds(at, tile), :]
                total = jnp.zeros((tile, 128), jnp.float32)
                for n in range(nc // 128):
                    part = cosine[:, n * 128 : (n + 1) * 128]
                    here = slice(c0 + n * 128, c0 + (n + 1) * 128)
                    same = column == lrow[j, 0:1, here]
                    if i == j and at < here.stop and here.start < at + tile:
                        mine = at + lax.broadcasted_iota(jnp.int32, (tile, 128), 0)
                        other = here.start + lax.broadcasted_iota(jnp.int32, (tile, 128), 1)
                        same = same & (mine != other)
                    term = jnp.where(same, jnp.exp2(part * SCALE - SCALE), 0.0)
                    total = total + term
                    if both:
                        csum[j, :, here] += jnp.sum(term.reshape(tile // 8, 8, 128), axis=0)
                rsum[i, pl.ds(at, tile), :] += total

    flag = jnp.max(jnp.where(lanes == FLAG_LANE, overflow, 0.0))
    mine = 2 * line_coord(c) + c
    for m in range(ND):
        line = jnp.sum(csum[m], axis=0, keepdims=True)
        if m < 4:
            line = line + jnp.sum(jnp.transpose(rsum[m]), axis=0, keepdims=True)
        line = jnp.broadcast_to(line, (8, BLK))
        for q in range(NQ):
            piece = (pltpu.roll(line, BLK - q * CAPB, axis=1) if q else line)[0:1, 0:128]
            ret[m, q] = jnp.where(lanes == FLAG_LANE, flag, piece)
    for m in range(ND):
        a, b = HELD[m]
        for q in range(NQ):
            if m == 0 and q == 0:
                pltpu.make_async_copy(ret.at[0, 0], got.at[0, mine], ret_in).start()
                continue
            dl, cs = q // 2, q % 2
            core = c if cs == 0 else 1 - c
            px = (x + c * (4 - a) + (1 - c) * dl) % 4
            pz = (z + (1 - c) * (4 - a) + c * dl) % 4
            py = (y + (4 - b) * (1 + 2 * c)) % 4
            remote(
                ret.at[m, q], got.at[m, mine], ret_out, ret_in, (px * 2 + core, pz * 4 + py)
            ).start()
    pltpu.make_async_copy(got, got, ret_in).wait()

    total = got[0, :, 0, :]
    for m in range(1, ND):
        total = total + got[m, :, 0, :]
    flag_ref[...] = jnp.max(jnp.where(tile_lane == FLAG_LANE, total, 0.0), keepdims=True)
    scores = jnp.log(1.0 + total)
    for n in range(docs // 128):
        here = slice(n * 128, (n + 1) * 128)
        spot = jnp.broadcast_to(jnp.minimum(rank[:, here], 127), (8, 128))
        picked = jnp.take_along_axis(scores, spot, axis=1)
        out_ref[:, here] = jnp.sum(
            jnp.where(tile_row == group[:, here], picked, 0.0), axis=0, keepdims=True
        )

    for copy in sent:
        copy.wait_send()
    most = ret.at[0, pl.ds(1, NQ - 1)]
    pltpu.make_async_copy(most, most, ret_out).wait()
    rest = ret.at[pl.ds(1, ND - 1)]
    pltpu.make_async_copy(rest, rest, ret_out).wait()


def fast(embeddings, cluster, slot):
    rows = embeddings.shape[0]
    dma = pltpu.SemaphoreType.DMA
    vmem = pl.BlockSpec(memory_space=pltpu.VMEM)
    return pl.pallas_call(
        score_kernel,
        out_shape=(
            jax.ShapeDtypeStruct((1, rows), jnp.float32),
            jax.ShapeDtypeStruct((1, 1), jnp.float32),
        ),
        in_specs=[vmem] * 3,
        out_specs=(vmem,) * 2,
        scratch_shapes=[
            pltpu.VMEM((NQ, CAPB, D), jnp.bfloat16),
            pltpu.VMEM((ND, BLK, D), jnp.bfloat16),
            pltpu.VMEM((ND, 8, BLK), jnp.float32),
            pltpu.VMEM((ND, BLK, 128), jnp.float32),
            pltpu.VMEM((4, BLK, 128), jnp.float32),
            pltpu.VMEM((ND, 8, BLK), jnp.float32),
            pltpu.VMEM((ND, NQ, 1, 128), jnp.float32),
            pltpu.VMEM((ND, 8, 1, 128), jnp.float32),
            dma((ND * NQ,)),
            dma(((ND - 1) * NQ,)),
            dma((NQ,)),
            dma(()),
            dma(()),
        ],
        compiler_params=pltpu.CompilerParams(
            collective_id=0, has_side_effects=True, vmem_limit_bytes=48 << 20
        ),
        name="scores",
    )(embeddings, slot.reshape(1, rows), cluster.reshape(1, rows))


def general(embeddings, cluster, slot):
    rows, width = embeddings.shape
    slots_dev = 2 * rows
    unit = (
        embeddings * lax.rsqrt(jnp.sum(embeddings * embeddings, axis=1, keepdims=True) + 1e-06)
    ).astype(jnp.bfloat16)
    both = ("group", "member")
    send_rows = jnp.zeros((slots_dev, width), jnp.bfloat16).at[slot].set(unit)
    send_labels = jnp.full((slots_dev,), -1, jnp.int32).at[slot].set(cluster)
    got_rows = lax.all_to_all(send_rows, both, split_axis=0, concat_axis=0, tiled=True)
    got_labels = lax.all_to_all(send_labels, both, split_axis=0, concat_axis=0, tiled=True)
    members = lax.axis_size("member")
    ring = [(i, (i + 1) % members) for i in range(members)]
    index = jnp.arange(slots_dev, dtype=jnp.int32)

    def step(turn, state):
        keys, labels, totals = state
        cosine = jnp.einsum("qd,kd->qk", got_rows, keys, preferred_element_type=jnp.float32)
        same = (got_labels[:, None] == labels[None, :]) & (labels[None, :] >= 0)
        same = same & ((index[:, None] != index[None, :]) | (turn > 0))
        terms = jnp.where(same, jnp.exp(20.0 * (cosine - 1.0)), jnp.float32(0.0))
        return (
            lax.ppermute(keys, "member", ring),
            lax.ppermute(labels, "member", ring),
            totals + jnp.sum(terms, axis=1),
        )

    zero = jnp.zeros((slots_dev,), jnp.float32)
    totals = lax.fori_loop(0, members, step, (got_rows, got_labels, zero))[2]
    scores = jnp.log(1.0 + totals)
    back = lax.all_to_all(scores, both, split_axis=0, concat_axis=0, tiled=True)
    return back[slot]


def body(embeddings, cluster, slot):
    out, flag = fast(embeddings, cluster, slot)
    return lax.cond(
        flag[0, 0] > 0.0,
        lambda: general(embeddings, cluster, slot),
        lambda: out.reshape(-1),
    )


def solution(mesh):
    spec = P(("group", "member"))
    in_specs = (P(("group", "member"), None), spec, spec)
    return jax.shard_map(body, mesh=mesh, in_specs=in_specs, out_specs=spec, check_vma=False)
```

```python
import functools
import math

import jax
import jax.numpy as jnp
from jax import lax
from jax.experimental import pallas as pl
from jax.experimental.pallas import tpu as pltpu
from jax.sharding import PartitionSpec as P

D = 768
CAPB = 96
DOCS = CAPB - 1
NQ = 8
BLK = NQ * CAPB
ND = 6
HALF = BLK // 2
TILE = 256
FLAG_LANE = 127
SCALE = 20.0 * math.log2(math.e)
MESH = pl.DeviceIdType.MESH
HELD = ((0, 0), (1, 0), (3, 0), (2, 0), (0, 1), (0, 2))

def turn(c, q):
    return (c if q % 2 == 0 else 1 - c), (4 - q // 2) % 4


def plan():
    steps = []

    def got(m, *chunks):
        steps.extend(("wait", m, q) for q in chunks)

    def spread(q):
        if q:
            got(0, q)
        steps.extend(("pass", m, 0, q) for m in (4, 1, 2))

    def pass5(*chunks):
        for q in chunks:
            got(4, q)
            steps.append(("pass", 5, 4, q))

    def pass3(*chunks):
        for q in chunks:
            got(1, q)
            got(2, q)
            steps.append(("pass", 3, 1 + q % 2, q))

    def names(m, *halves):
        steps.extend(("names", m, h) for h in halves)

    def product(i, rows, j, cols, sums):
        steps.append(("product", i, rows, j, cols, sums))

    whole, first, second = (0, BLK), (0, HALF), (HALF, HALF)
    steps.append(("pack", (2, 3, 1, 0)))
    steps.append(("meet",))
    steps.extend(("route", q) for q in (1, 2, 3))
    spread(0)
    steps.append(("pack", (6, 7, 4, 5)))
    steps.extend(("route", q) for q in (6, 7, 4, 5))
    spread(1)
    pass5(0)
    for q in (2, 3, 6, 7, 4, 5):
        spread(q)
    pass5(1, 2, 3)
    names(0, 0, 1)
    product(0, whole, 0, whole, "rows")
    pass3(0, 1, 2, 3)
    names(4, 0)
    names(1, 0)
    names(2, 0)
    product(0, whole, 4, first, "both")
    product(0, whole, 1, first, "both")
    pass5(6, 7)
    product(1, first, 4, first, "both")
    product(2, first, 4, first, "both")
    pass3(6, 7)
    pass5(4, 5)
    names(4, 1)
    product(0, whole, 4, second, "both")
    pass3(4, 5)
    names(1, 1)
    names(2, 1)
    product(0, whole, 1, second, "both")
    for m in (2, 1):
        product(m, second, 4, first, "both")
        product(m, whole, 4, second, "both")
    steps.append(("return", ((2, range(NQ)),)))
    got(5, 0, 1, 2, 3)
    names(5, 0)
    product(0, whole, 5, first, "rows")
    product(1, whole, 5, first, "both")
    got(3, 0, 1, 2, 3)
    names(3, 0)
    product(0, whole, 3, first, "rows")
    product(3, first, 4, whole, "both")
    product(3, first, 5, first, "rows")
    got(3, 6, 7, 4, 5)
    names(3, 1)
    product(0, whole, 3, second, "rows")
    product(3, second, 4, whole, "both")
    product(3, second, 5, first, "cols")
    steps.append(("return", ((3, range(NQ)), (4, range(NQ)), (5, range(4)))))
    got(5, 6, 7, 4, 5)
    names(5, 1)
    product(0, whole, 5, second, "rows")
    product(1, whole, 5, second, "both")
    product(3, whole, 5, second, "cols")
    steps.append(("return", ((5, range(4, NQ)), (1, range(NQ)), (0, range(NQ)))))
    return steps


def score_kernel(
    emb_ref,
    slot_ref,
    clu_ref,
    out_ref,
    flag_ref,
    held,
    unit,
    send,
    blk,
    lrow,
    lcol,
    rsum,
    csum,
    ret,
    got,
    emb_sem,
    arr_sem,
    out_sem,
    p1_out,
    ret_in,
    ret_out,
):
    gi = lax.axis_index("group")
    mi = lax.axis_index("member")
    x, c = gi // 2, gi % 2
    z, y = mi // 4, mi % 4

    def line_coord(t):
        return x * (1 - t) + z * t

    def line_dev(t, off, core):
        return (((x + (1 - t) * off) % 4) * 2 + core, ((z + t * off) % 4) * 4 + y)

    def plane_dev(a, b):
        px = (x + c * a) % 4
        pz = (z + (1 - c) * a) % 4
        py = (y + b * (1 + 2 * c)) % 4
        return (px * 2 + c, pz * 4 + py)

    def remote(src, dst, send_sem, recv_sem, dev):
        return pltpu.make_async_remote_copy(
            src_ref=src,
            dst_ref=dst,
            send_sem=send_sem,
            recv_sem=recv_sem,
            device_id=dev,
            device_id_type=MESH,
        )

    def chunk(m, q):
        return blk.at[m, pl.ds(q * CAPB, CAPB), :]

    barrier = pltpu.get_barrier_semaphore()
    partners = [(x * 2 + 1 - c, mi)]
    for off in (1, 2, 3):
        partners += [line_dev(c, off, c), line_dev(1 - c, off, 1 - c), line_dev(c, off, 1 - c)]
    partners += [plane_dev(1, 0), plane_dev(3, 0), plane_dev(0, 1), plane_dev(0, 3)]
    for dev in partners:
        pl.semaphore_signal(barrier, inc=1, device_id=dev, device_id_type=MESH)

    docs = emb_ref.shape[0]
    step_rows = docs // 4
    loads = []
    for k in range(4):
        rows = pl.ds(k * step_rows, step_rows)
        loads.append(pltpu.make_async_copy(emb_ref.at[rows], held.at[rows], emb_sem.at[k]))
        loads[k].start()

    group = slot_ref[...] // 128
    ids = lax.broadcasted_iota(jnp.int32, (8, docs), 0)
    member = (ids == group).astype(jnp.float32)
    upper = lax.broadcasted_iota(jnp.int32, (docs, docs), 0) < lax.broadcasted_iota(
        jnp.int32, (docs, docs), 1
    )
    before = jnp.dot(
        member.astype(jnp.bfloat16),
        upper.astype(jnp.float32).astype(jnp.bfloat16),
        preferred_element_type=jnp.float32,
    )
    rank = jnp.sum(member * before, axis=0, keepdims=True).astype(jnp.int32)
    fits = rank < DOCS
    place = jnp.where(fits, group * CAPB + rank, -1)

    lane = lax.broadcasted_iota(jnp.int32, (128, docs), 0)
    at_rank = ((lane == rank) & fits).astype(jnp.float32).astype(jnp.bfloat16)
    label = (member * (clu_ref[...] + 1).astype(jnp.float32)).astype(jnp.bfloat16)
    labels = lax.dot_general(
        label, at_rank, (((1,), (1,)), ((), ())), preferred_element_type=jnp.float32
    )
    tile_lane = lax.broadcasted_iota(jnp.int32, (8, 128), 1)
    tile_row = lax.broadcasted_iota(jnp.int32, (8, 128), 0)
    labels = jnp.where(tile_lane == FLAG_LANE, jnp.max(jnp.where(fits, 0.0, 1.0)), labels)

    rsum[...] = jnp.zeros_like(rsum)
    csum[...] = jnp.zeros_like(csum)
    for k in range(4):
        rows = pl.ds(k * step_rows, step_rows)
        loads[k].wait()
        values = held[rows, :]
        squares = jnp.sum(values * values, axis=1, keepdims=True)
        unit[rows, :] = (values * lax.rsqrt(squares + 1e-06)).astype(jnp.bfloat16)

    row = lax.broadcasted_iota(jnp.int32, (CAPB, docs), 0)
    last = lax.broadcasted_iota(jnp.int32, (CAPB, 128), 0) == DOCS

    def pack(chunks):
        owners = []
        for q in chunks:
            t, off = turn(c, q)
            owners.append(2 * ((line_coord(t) + off) % 4) + t)
        chosen = jnp.concatenate(
            [(row + g * CAPB == place).astype(jnp.float32) for g in owners], axis=0
        ).astype(jnp.bfloat16)
        packed = jnp.dot(chosen, unit[...], preferred_element_type=jnp.float32)
        for k, (q, g) in enumerate(zip(chunks, owners)):
            part = packed[k * CAPB : (k + 1) * CAPB]
            tail = jnp.sum(jnp.where(tile_row == g, labels, 0.0), axis=0, keepdims=True)
            part = jnp.concatenate([jnp.where(last, tail, part[:, :128]), part[:, 128:]], axis=1)
            if q:
                send[q] = part.astype(jnp.bfloat16)
            else:
                blk[0, 0:CAPB, :] = part.astype(jnp.bfloat16)

    sent = []

    def start(copy):
        copy.start()
        sent.append(copy)

    lanes = lax.broadcasted_iota(jnp.int32, (1, 128), 1)
    overflow = jnp.zeros((1, 128), jnp.float32)
    hops = {1: plane_dev(1, 0), 2: plane_dev(3, 0), 4: plane_dev(0, 1), 5: plane_dev(0, 1)}

    home = 2 * line_coord(c) + c

    def give_back(blocks, seen):
        flag = jnp.max(jnp.where(lanes == FLAG_LANE, seen, 0.0))
        for m, chunks in blocks:
            line = jnp.sum(csum[m], axis=0, keepdims=True)
            if m < 4:
                line = line + jnp.sum(jnp.transpose(rsum[m]), axis=0, keepdims=True)
            line = jnp.broadcast_to(line, (8, BLK))
            for q in chunks:
                piece = (pltpu.roll(line, BLK - q * CAPB, axis=1) if q else line)[0:1, 0:128]
                ret[m, q] = jnp.where(lanes == FLAG_LANE, flag, piece)
        for m, chunks in blocks:
            a, b = HELD[m]
            for q in chunks:
                if m == 0 and q == 0:
                    pltpu.make_async_copy(ret.at[0, 0], got.at[0, home], ret_in).start()
                    continue
                dl, cs = q // 2, q % 2
                core = c if cs == 0 else 1 - c
                px = (x + c * (4 - a) + (1 - c) * dl) % 4
                pz = (z + (1 - c) * (4 - a) + c * dl) % 4
                py = (y + (4 - b) * (1 + 2 * c)) % 4
                remote(
                    ret.at[m, q], got.at[m, home], ret_out, ret_in, (px * 2 + core, pz * 4 + py)
                ).start()

    for step in plan():
        if step[0] == "pack":
            pack(step[1])
        elif step[0] == "meet":
            pl.semaphore_wait(barrier, len(partners))
        elif step[0] == "return":
            give_back(step[1], overflow)
        elif step[0] == "route":
            q = step[1]
            t, off = turn(c, q)
            start(remote(send.at[q], chunk(0, q), p1_out.at[q], arr_sem.at[q], line_dev(t, off, t)))
        elif step[0] == "pass":
            _, m, src, q = step
            start(
                remote(
                    chunk(src, q), chunk(m, q), out_sem.at[(m - 1) * NQ + q],
                    arr_sem.at[m * NQ + q], hops[src if m == 3 else m],
                )
            )
        elif step[0] == "wait":
            _, m, q = step
            pltpu.make_async_copy(chunk(m, q), chunk(m, q), arr_sem.at[m * NQ + q]).wait()
        elif step[0] == "names":
            _, m, h = step
            rows = []
            for q in range(4 * h, 4 * h + 4):
                tail = blk[m, pl.ds(q * CAPB + CAPB - 16, 16), 0:128].astype(jnp.float32)
                rows.append(tail[15:16, :])
            found = jnp.concatenate(rows + [jnp.zeros((4, 128), jnp.float32)], axis=0)
            overflow = jnp.maximum(overflow, jnp.max(found, axis=0, keepdims=True))
            found = jnp.where(lanes < DOCS, found, 0.0)
            wide = jnp.zeros((8, HALF), jnp.float32)
            for k in range(4):
                piece = jnp.concatenate(
                    [
                        jnp.broadcast_to(found[k : k + 1, :], (8, 128)),
                        jnp.zeros((8, HALF - 128), jnp.float32),
                    ],
                    axis=1,
                )
                wide = wide + (pltpu.roll(piece, k * CAPB, axis=1) if k else piece)
            lrow[m, :, h * HALF : (h + 1) * HALF] = wide
            turned = jnp.transpose(
                jnp.concatenate([found, jnp.zeros((120, 128), jnp.float32)], axis=0)
            )
            for k in range(4):
                column = jnp.broadcast_to(turned[0:CAPB, k : k + 1], (CAPB, 128))
                lcol[m, pl.ds(h * HALF + k * CAPB, CAPB), :] = jnp.where(
                    column == 0.0, -1.0, column
                )
        else:
            _, i, (r0, nr), j, (c0, nc), sums = step
            tile = TILE if nr % TILE == 0 else nr
            for at in range(r0, r0 + nr, tile):
                cosine = lax.dot_general(
                    blk[i, pl.ds(at, tile), :],
                    blk[j, pl.ds(c0, nc), :],
                    (((1,), (1,)), ((), ())),
                    preferred_element_type=jnp.float32,
                )
                column = lcol[i, pl.ds(at, tile), :]
                total = jnp.zeros((tile, 128), jnp.float32)
                for n in range(nc // 128):
                    part = cosine[:, n * 128 : (n + 1) * 128]
                    here = slice(c0 + n * 128, c0 + (n + 1) * 128)
                    same = column == lrow[j, 0:1, here]
                    if i == j and at < here.stop and here.start < at + tile:
                        mine = at + lax.broadcasted_iota(jnp.int32, (tile, 128), 0)
                        other = here.start + lax.broadcasted_iota(jnp.int32, (tile, 128), 1)
                        same = same & (mine != other)
                    term = jnp.where(same, jnp.exp2(part * SCALE - SCALE), 0.0)
                    if sums != "cols":
                        total = total + term
                    if sums != "rows":
                        csum[j, :, here] += jnp.sum(term.reshape(tile // 8, 8, 128), axis=0)
                if sums != "cols":
                    rsum[i, pl.ds(at, tile), :] += total

    pltpu.make_async_copy(got, got, ret_in).wait()

    total = got[0, :, 0, :]
    for m in range(1, ND):
        total = total + got[m, :, 0, :]
    flag_ref[...] = jnp.max(jnp.where(tile_lane == FLAG_LANE, total, 0.0), keepdims=True)
    scores = jnp.log(1.0 + total)
    for n in range(docs // 128):
        here = slice(n * 128, (n + 1) * 128)
        spot = jnp.broadcast_to(jnp.minimum(rank[:, here], 127), (8, 128))
        picked = jnp.take_along_axis(scores, spot, axis=1)
        out_ref[:, here] = jnp.sum(
            jnp.where(tile_row == group[:, here], picked, 0.0), axis=0, keepdims=True
        )

    for copy in sent:
        copy.wait_send()
    most = ret.at[0, pl.ds(1, NQ - 1)]
    pltpu.make_async_copy(most, most, ret_out).wait()
    rest = ret.at[pl.ds(1, ND - 1)]
    pltpu.make_async_copy(rest, rest, ret_out).wait()


def fast(embeddings, cluster, slot):
    rows = embeddings.shape[0]
    dma = pltpu.SemaphoreType.DMA
    vmem = pl.BlockSpec(memory_space=pltpu.VMEM)
    return pl.pallas_call(
        score_kernel,
        out_shape=(
            jax.ShapeDtypeStruct((1, rows), jnp.float32),
            jax.ShapeDtypeStruct((1, 1), jnp.float32),
        ),
        in_specs=[pl.BlockSpec(memory_space=pl.ANY), vmem, vmem],
        out_specs=(vmem,) * 2,
        scratch_shapes=[
            pltpu.VMEM((rows, D), jnp.float32),
            pltpu.VMEM((rows, D), jnp.bfloat16),
            pltpu.VMEM((NQ, CAPB, D), jnp.bfloat16),
            pltpu.VMEM((ND, BLK, D), jnp.bfloat16),
            pltpu.VMEM((ND, 8, BLK), jnp.float32),
            pltpu.VMEM((ND, BLK, 128), jnp.float32),
            pltpu.VMEM((4, BLK, 128), jnp.float32),
            pltpu.VMEM((ND, 8, BLK), jnp.float32),
            pltpu.VMEM((ND, NQ, 1, 128), jnp.float32),
            pltpu.VMEM((ND, 8, 1, 128), jnp.float32),
            dma((4,)),
            dma((ND * NQ,)),
            dma(((ND - 1) * NQ,)),
            dma((NQ,)),
            dma(()),
            dma(()),
        ],
        compiler_params=pltpu.CompilerParams(
            collective_id=0, has_side_effects=True, vmem_limit_bytes=48 << 20
        ),
        name="scores",
    )(embeddings, slot.reshape(1, rows), cluster.reshape(1, rows))


def general(embeddings, cluster, slot):
    rows, width = embeddings.shape
    slots_dev = 2 * rows
    unit = (
        embeddings * lax.rsqrt(jnp.sum(embeddings * embeddings, axis=1, keepdims=True) + 1e-06)
    ).astype(jnp.bfloat16)
    both = ("group", "member")
    send_rows = jnp.zeros((slots_dev, width), jnp.bfloat16).at[slot].set(unit)
    send_labels = jnp.full((slots_dev,), -1, jnp.int32).at[slot].set(cluster)
    got_rows = lax.all_to_all(send_rows, both, split_axis=0, concat_axis=0, tiled=True)
    got_labels = lax.all_to_all(send_labels, both, split_axis=0, concat_axis=0, tiled=True)
    members = lax.axis_size("member")
    ring = [(i, (i + 1) % members) for i in range(members)]
    index = jnp.arange(slots_dev, dtype=jnp.int32)

    def step(turn, state):
        keys, labels, totals = state
        cosine = jnp.einsum("qd,kd->qk", got_rows, keys, preferred_element_type=jnp.float32)
        same = (got_labels[:, None] == labels[None, :]) & (labels[None, :] >= 0)
        same = same & ((index[:, None] != index[None, :]) | (turn > 0))
        terms = jnp.where(same, jnp.exp(20.0 * (cosine - 1.0)), jnp.float32(0.0))
        return (
            lax.ppermute(keys, "member", ring),
            lax.ppermute(labels, "member", ring),
            totals + jnp.sum(terms, axis=1),
        )

    zero = jnp.zeros((slots_dev,), jnp.float32)
    totals = lax.fori_loop(0, members, step, (got_rows, got_labels, zero))[2]
    scores = jnp.log(1.0 + totals)
    back = lax.all_to_all(scores, both, split_axis=0, concat_axis=0, tiled=True)
    return back[slot]


def body(embeddings, cluster, slot):
    out, flag = fast(embeddings, cluster, slot)
    return lax.cond(
        flag[0, 0] > 0.0,
        lambda: general(embeddings, cluster, slot),
        lambda: out.reshape(-1),
    )


def solution(mesh):
    spec = P(("group", "member"))
    in_specs = (P(("group", "member"), None), spec, spec)
    return jax.shard_map(body, mesh=mesh, in_specs=in_specs, out_specs=spec, check_vma=False)
```

```python
import functools
import math

import jax
import jax.numpy as jnp
from jax import lax
from jax.experimental import pallas as pl
from jax.experimental.pallas import tpu as pltpu
from jax.sharding import PartitionSpec as P

D = 768
CAPB = 96
DOCS = CAPB - 1
NQ = 8
BLK = NQ * CAPB
ND = 6
HALF = BLK // 2
TILE = 256
FLAG_LANE = 127
SCALE = 20.0 * math.log2(math.e)
MESH = pl.DeviceIdType.MESH
HELD = ((0, 0), (1, 0), (3, 0), (2, 0), (0, 1), (0, 2))

def turn(c, q):
    return (c if q % 2 == 0 else 1 - c), (4 - q // 2) % 4


def plan():
    steps = []

    def got(m, *chunks):
        steps.extend(("wait", m, q) for q in chunks)

    def spread(q):
        if q:
            got(0, q)
        steps.extend(("pass", m, 0, q) for m in (4, 1, 2))

    def pass5(*chunks):
        for q in chunks:
            got(4, q)
            steps.append(("pass", 5, 4, q))

    def pass3(*chunks):
        for q in chunks:
            got(1, q)
            got(2, q)
            steps.append(("pass", 3, 1 + q % 2, q))

    def names(m, *halves):
        steps.extend(("names", m, h) for h in halves)

    def product(i, rows, j, cols, sums):
        steps.append(("product", i, rows, j, cols, sums))

    whole, first, second = (0, BLK), (0, HALF), (HALF, HALF)
    steps.append(("pack", (2, 3, 1, 0)))
    steps.append(("meet",))
    steps.extend(("route", q) for q in (1, 2, 3))
    spread(0)
    steps.append(("pack", (6, 7, 4, 5)))
    steps.extend(("route", q) for q in (6, 7, 4, 5))
    spread(1)
    pass5(0)
    for q in (2, 3, 6, 7, 4, 5):
        spread(q)
    pass5(1, 2, 3)
    names(0, 0, 1)
    product(0, whole, 0, whole, "rows")
    pass3(0, 1, 2, 3)
    names(4, 0)
    names(1, 0)
    names(2, 0)
    product(0, whole, 4, first, "both")
    product(0, whole, 1, first, "both")
    pass5(6, 7)
    product(1, first, 4, first, "both")
    product(2, first, 4, first, "both")
    pass3(6, 7)
    pass5(4, 5)
    names(4, 1)
    product(0, whole, 4, second, "both")
    pass3(4, 5)
    names(1, 1)
    names(2, 1)
    product(0, whole, 1, second, "both")
    for m in (2, 1):
        product(m, second, 4, first, "both")
        product(m, whole, 4, second, "both")
    steps.append(("return", ((2, range(NQ)),)))
    got(5, 0, 1, 2, 3)
    names(5, 0)
    product(0, whole, 5, first, "rows")
    product(1, whole, 5, first, "both")
    got(3, 0, 1, 2, 3)
    names(3, 0)
    product(0, whole, 3, first, "rows")
    product(3, first, 4, whole, "both")
    product(3, first, 5, first, "rows")
    got(3, 6, 7, 4, 5)
    names(3, 1)
    product(0, whole, 3, second, "rows")
    product(3, second, 4, whole, "both")
    product(3, second, 5, first, "cols")
    steps.append(("return", ((3, range(NQ)), (4, range(NQ)), (5, range(4)))))
    got(5, 6, 7, 4, 5)
    names(5, 1)
    product(0, whole, 5, second, "rows")
    product(1, whole, 5, second, "both")
    product(3, whole, 5, second, "cols")
    steps.append(("return", ((5, range(4, NQ)), (1, range(NQ)), (0, range(NQ)))))
    return steps


def score_kernel(
    emb_ref,
    slot_ref,
    clu_ref,
    out_ref,
    flag_ref,
    held,
    unit,
    send,
    blk,
    lrow,
    lcol,
    rsum,
    csum,
    ret,
    got,
    emb_sem,
    arr_sem,
    out_sem,
    p1_out,
    ret_in,
    ret_out,
):
    gi = lax.axis_index("group")
    mi = lax.axis_index("member")
    x, c = gi // 2, gi % 2
    z, y = mi // 4, mi % 4

    def line_coord(t):
        return x * (1 - t) + z * t

    def line_dev(t, off, core):
        return (((x + (1 - t) * off) % 4) * 2 + core, ((z + t * off) % 4) * 4 + y)

    def plane_dev(a, b):
        px = (x + c * a) % 4
        pz = (z + (1 - c) * a) % 4
        py = (y + b * (1 + 2 * c)) % 4
        return (px * 2 + c, pz * 4 + py)

    def remote(src, dst, send_sem, recv_sem, dev):
        return pltpu.make_async_remote_copy(
            src_ref=src,
            dst_ref=dst,
            send_sem=send_sem,
            recv_sem=recv_sem,
            device_id=dev,
            device_id_type=MESH,
        )

    def chunk(m, q):
        return blk.at[m, pl.ds(q * CAPB, CAPB), :]

    barrier = pltpu.get_barrier_semaphore()
    partners = [(x * 2 + 1 - c, mi)]
    for off in (1, 2, 3):
        partners += [line_dev(c, off, c), line_dev(1 - c, off, 1 - c), line_dev(c, off, 1 - c)]
    partners += [plane_dev(1, 0), plane_dev(3, 0), plane_dev(0, 1), plane_dev(0, 3)]
    for dev in partners:
        pl.semaphore_signal(barrier, inc=1, device_id=dev, device_id_type=MESH)

    docs = emb_ref.shape[0]
    step_rows = docs // 4
    loads = []
    for k in range(4):
        rows = pl.ds(k * step_rows, step_rows)
        loads.append(pltpu.make_async_copy(emb_ref.at[rows], held.at[rows], emb_sem.at[k]))
        loads[k].start()

    group = slot_ref[...] // 128
    ids = lax.broadcasted_iota(jnp.int32, (8, docs), 0)
    member = (ids == group).astype(jnp.float32)
    upper = lax.broadcasted_iota(jnp.int32, (docs, docs), 0) < lax.broadcasted_iota(
        jnp.int32, (docs, docs), 1
    )
    before = jnp.dot(
        member.astype(jnp.bfloat16),
        upper.astype(jnp.float32).astype(jnp.bfloat16),
        preferred_element_type=jnp.float32,
    )
    rank = jnp.sum(member * before, axis=0, keepdims=True).astype(jnp.int32)
    fits = rank < DOCS
    place = jnp.where(fits, group * CAPB + rank, -1)

    lane = lax.broadcasted_iota(jnp.int32, (128, docs), 0)
    at_rank = ((lane == rank) & fits).astype(jnp.float32).astype(jnp.bfloat16)
    label = (member * (clu_ref[...] + 1).astype(jnp.float32)).astype(jnp.bfloat16)
    labels = lax.dot_general(
        label, at_rank, (((1,), (1,)), ((), ())), preferred_element_type=jnp.float32
    )
    tile_lane = lax.broadcasted_iota(jnp.int32, (8, 128), 1)
    tile_row = lax.broadcasted_iota(jnp.int32, (8, 128), 0)
    labels = jnp.where(tile_lane == FLAG_LANE, jnp.max(jnp.where(fits, 0.0, 1.0)), labels)

    rsum[...] = jnp.zeros_like(rsum)
    csum[...] = jnp.zeros_like(csum)
    for k in range(4):
        rows = pl.ds(k * step_rows, step_rows)
        loads[k].wait()
        values = held[rows, :]
        squares = jnp.sum(values * values, axis=1, keepdims=True)
        unit[rows, :] = (values * lax.rsqrt(squares + 1e-06)).astype(jnp.bfloat16)

    row = lax.broadcasted_iota(jnp.int32, (CAPB, docs), 0)
    last = lax.broadcasted_iota(jnp.int32, (CAPB, 128), 0) == DOCS

    def pack(chunks):
        owners = []
        for q in chunks:
            t, off = turn(c, q)
            owners.append(2 * ((line_coord(t) + off) % 4) + t)
        chosen = jnp.concatenate(
            [(row + g * CAPB == place).astype(jnp.float32) for g in owners], axis=0
        ).astype(jnp.bfloat16)
        packed = jnp.dot(chosen, unit[...], preferred_element_type=jnp.float32)
        for k, (q, g) in enumerate(zip(chunks, owners)):
            part = packed[k * CAPB : (k + 1) * CAPB]
            tail = jnp.sum(jnp.where(tile_row == g, labels, 0.0), axis=0, keepdims=True)
            part = jnp.concatenate([jnp.where(last, tail, part[:, :128]), part[:, 128:]], axis=1)
            if q:
                send[q] = part.astype(jnp.bfloat16)
            else:
                blk[0, 0:CAPB, :] = part.astype(jnp.bfloat16)

    sent = []

    def start(copy):
        copy.start()
        sent.append(copy)

    lanes = lax.broadcasted_iota(jnp.int32, (1, 128), 1)
    overflow = jnp.zeros((1, 128), jnp.float32)
    hops = {1: plane_dev(1, 0), 2: plane_dev(3, 0), 4: plane_dev(0, 1), 5: plane_dev(0, 1)}

    home = 2 * line_coord(c) + c

    def give_back(blocks, seen):
        flag = jnp.max(jnp.where(lanes == FLAG_LANE, seen, 0.0))
        for m, chunks in blocks:
            line = jnp.sum(csum[m], axis=0, keepdims=True)
            if m < 4:
                line = line + jnp.sum(jnp.transpose(rsum[m]), axis=0, keepdims=True)
            line = jnp.broadcast_to(line, (8, BLK))
            for q in chunks:
                piece = (pltpu.roll(line, BLK - q * CAPB, axis=1) if q else line)[0:1, 0:128]
                ret[m, q] = jnp.where(lanes == FLAG_LANE, flag, piece)
        for m, chunks in blocks:
            a, b = HELD[m]
            for q in chunks:
                if m == 0 and q == 0:
                    pltpu.make_async_copy(ret.at[0, 0], got.at[0, home], ret_in).start()
                    continue
                dl, cs = q // 2, q % 2
                core = c if cs == 0 else 1 - c
                px = (x + c * (4 - a) + (1 - c) * dl) % 4
                pz = (z + (1 - c) * (4 - a) + c * dl) % 4
                py = (y + (4 - b) * (1 + 2 * c)) % 4
                remote(
                    ret.at[m, q], got.at[m, home], ret_out, ret_in, (px * 2 + core, pz * 4 + py)
                ).start()

    for step in plan():
        if step[0] == "pack":
            pack(step[1])
        elif step[0] == "meet":
            pl.semaphore_wait(barrier, len(partners))
        elif step[0] == "return":
            give_back(step[1], overflow)
        elif step[0] == "route":
            q = step[1]
            t, off = turn(c, q)
            start(remote(send.at[q], chunk(0, q), p1_out.at[q], arr_sem.at[q], line_dev(t, off, t)))
        elif step[0] == "pass":
            _, m, src, q = step
            start(
                remote(
                    chunk(src, q), chunk(m, q), out_sem.at[(m - 1) * NQ + q],
                    arr_sem.at[m * NQ + q], hops[src if m == 3 else m],
                )
            )
        elif step[0] == "wait":
            _, m, q = step
            pltpu.make_async_copy(chunk(m, q), chunk(m, q), arr_sem.at[m * NQ + q]).wait()
        elif step[0] == "names":
            _, m, h = step
            rows = []
            for q in range(4 * h, 4 * h + 4):
                tail = blk[m, pl.ds(q * CAPB + CAPB - 16, 16), 0:128].astype(jnp.float32)
                rows.append(tail[15:16, :])
            found = jnp.concatenate(rows + [jnp.zeros((4, 128), jnp.float32)], axis=0)
            overflow = jnp.maximum(overflow, jnp.max(found, axis=0, keepdims=True))
            found = jnp.where(lanes < DOCS, found, 0.0)
            wide = jnp.zeros((8, HALF), jnp.float32)
            for k in range(4):
                piece = jnp.concatenate(
                    [
                        jnp.broadcast_to(found[k : k + 1, :], (8, 128)),
                        jnp.zeros((8, HALF - 128), jnp.float32),
                    ],
                    axis=1,
                )
                wide = wide + (pltpu.roll(piece, k * CAPB, axis=1) if k else piece)
            lrow[m, :, h * HALF : (h + 1) * HALF] = wide
            turned = jnp.transpose(
                jnp.concatenate([found, jnp.zeros((120, 128), jnp.float32)], axis=0)
            )
            for k in range(4):
                column = jnp.broadcast_to(turned[0:CAPB, k : k + 1], (CAPB, 128))
                lcol[m, pl.ds(h * HALF + k * CAPB, CAPB), :] = jnp.where(
                    column == 0.0, -1.0, column
                )
        else:
            _, i, (r0, nr), j, (c0, nc), sums = step
            tile = TILE if nr % TILE == 0 else nr
            for at in range(r0, r0 + nr, tile):
                cosine = lax.dot_general(
                    blk[i, pl.ds(at, tile), :],
                    blk[j, pl.ds(c0, nc), :],
                    (((1,), (1,)), ((), ())),
                    preferred_element_type=jnp.float32,
                )
                column = lcol[i, pl.ds(at, tile), :]
                total = jnp.zeros((tile, 128), jnp.float32)
                for n in range(nc // 128):
                    part = cosine[:, n * 128 : (n + 1) * 128]
                    here = slice(c0 + n * 128, c0 + (n + 1) * 128)
                    same = column == lrow[j, 0:1, here]
                    if i == j and at < here.stop and here.start < at + tile:
                        mine = at + lax.broadcasted_iota(jnp.int32, (tile, 128), 0)
                        other = here.start + lax.broadcasted_iota(jnp.int32, (tile, 128), 1)
                        same = same & (mine != other)
                    term = jnp.where(same, jnp.exp2(part * SCALE - SCALE), 0.0)
                    if sums != "cols":
                        total = total + term
                    if sums != "rows":
                        csum[j, :, here] += jnp.sum(term.reshape(tile // 8, 8, 128), axis=0)
                if sums != "cols":
                    rsum[i, pl.ds(at, tile), :] += total

    pltpu.make_async_copy(got, got, ret_in).wait()

    total = got[0, :, 0, :]
    for m in range(1, ND):
        total = total + got[m, :, 0, :]
    flag_ref[...] = jnp.max(jnp.where(tile_lane == FLAG_LANE, total, 0.0), keepdims=True)
    scores = jnp.log(1.0 + total)
    for n in range(docs // 128):
        here = slice(n * 128, (n + 1) * 128)
        spot = jnp.broadcast_to(jnp.minimum(rank[:, here], 127), (8, 128))
        picked = jnp.take_along_axis(scores, spot, axis=1)
        out_ref[:, here] = jnp.sum(
            jnp.where(tile_row == group[:, here], picked, 0.0), axis=0, keepdims=True
        )

    for copy in sent:
        copy.wait_send()
    most = ret.at[0, pl.ds(1, NQ - 1)]
    pltpu.make_async_copy(most, most, ret_out).wait()
    rest = ret.at[pl.ds(1, ND - 1)]
    pltpu.make_async_copy(rest, rest, ret_out).wait()


def fast(embeddings, cluster, slot):
    rows = embeddings.shape[0]
    dma = pltpu.SemaphoreType.DMA
    vmem = pl.BlockSpec(memory_space=pltpu.VMEM)
    return pl.pallas_call(
        score_kernel,
        out_shape=(
            jax.ShapeDtypeStruct((1, rows), jnp.float32),
            jax.ShapeDtypeStruct((1, 1), jnp.float32),
        ),
        in_specs=[pl.BlockSpec(memory_space=pl.ANY), vmem, vmem],
        out_specs=(vmem,) * 2,
        scratch_shapes=[
            pltpu.VMEM((rows, D), jnp.float32),
            pltpu.VMEM((rows, D), jnp.bfloat16),
            pltpu.VMEM((NQ, CAPB, D), jnp.bfloat16),
            pltpu.VMEM((ND, BLK, D), jnp.bfloat16),
            pltpu.VMEM((ND, 8, BLK), jnp.float32),
            pltpu.VMEM((ND, BLK, 128), jnp.float32),
            pltpu.VMEM((4, BLK, 128), jnp.float32),
            pltpu.VMEM((ND, 8, BLK), jnp.float32),
            pltpu.VMEM((ND, NQ, 1, 128), jnp.float32),
            pltpu.VMEM((ND, 8, 1, 128), jnp.float32),
            dma((4,)),
            dma((ND * NQ,)),
            dma(((ND - 1) * NQ,)),
            dma((NQ,)),
            dma(()),
            dma(()),
        ],
        compiler_params=pltpu.CompilerParams(
            collective_id=0, has_side_effects=True, vmem_limit_bytes=48 << 20
        ),
        name="scores",
    )(embeddings, slot.reshape(1, rows), cluster.reshape(1, rows))


def general(embeddings, cluster, slot):
    rows, width = embeddings.shape
    slots_dev = 2 * rows
    unit = (
        embeddings * lax.rsqrt(jnp.sum(embeddings * embeddings, axis=1, keepdims=True) + 1e-06)
    ).astype(jnp.bfloat16)
    both = ("group", "member")
    send_rows = jnp.zeros((slots_dev, width), jnp.bfloat16).at[slot].set(unit)
    send_labels = jnp.full((slots_dev,), -1, jnp.int32).at[slot].set(cluster)
    got_rows = lax.all_to_all(send_rows, both, split_axis=0, concat_axis=0, tiled=True)
    got_labels = lax.all_to_all(send_labels, both, split_axis=0, concat_axis=0, tiled=True)
    members = lax.axis_size("member")
    me = lax.axis_index("member")
    everyone = jnp.broadcast_to(got_rows[None], (members, slots_dev, width))
    keys = lax.all_to_all(everyone, "member", split_axis=0, concat_axis=0)
    names = jnp.broadcast_to(got_labels[None], (members, slots_dev))
    key_labels = lax.all_to_all(names, "member", split_axis=0, concat_axis=0)
    index = jnp.arange(slots_dev, dtype=jnp.int32)

    def step(k, totals):
        cosine = jnp.einsum("qd,kd->qk", got_rows, keys[k], preferred_element_type=jnp.float32)
        labels = key_labels[k]
        same = (got_labels[:, None] == labels[None, :]) & (labels[None, :] >= 0)
        same = same & (me * slots_dev + index[:, None] != k * slots_dev + index[None, :])
        terms = jnp.where(same, jnp.exp(20.0 * (cosine - 1.0)), jnp.float32(0.0))
        return totals + jnp.sum(terms, axis=1)

    totals = lax.fori_loop(0, members, step, jnp.zeros((slots_dev,), jnp.float32))
    scores = jnp.log(1.0 + totals)
    back = lax.all_to_all(scores, both, split_axis=0, concat_axis=0, tiled=True)
    return back[slot]


def body(embeddings, cluster, slot):
    out, flag = fast(embeddings, cluster, slot)
    return lax.cond(
        flag[0, 0] > 0.0,
        lambda: general(embeddings, cluster, slot),
        lambda: out.reshape(-1),
    )


def solution(mesh):
    spec = P(("group", "member"))
    in_specs = (P(("group", "member"), None), spec, spec)
    return jax.shard_map(body, mesh=mesh, in_specs=in_specs, out_specs=spec, check_vma=False)
```

```python
import functools
import math

import jax
import jax.numpy as jnp
from jax import lax
from jax.experimental import pallas as pl
from jax.experimental.pallas import tpu as pltpu
from jax.sharding import PartitionSpec as P

D = 768
CAPB = 96
DOCS = CAPB - 1
NQ = 8
BLK = NQ * CAPB
ND = 6
HALF = BLK // 2
TILE = 256
FLAG_LANE = 127
SCALE = 20.0 * math.log2(math.e)
MESH = pl.DeviceIdType.MESH
HELD = ((0, 0), (1, 0), (3, 0), (2, 0), (0, 1), (0, 2))

def turn(c, q):
    return (c if q % 2 == 0 else 1 - c), (4 - q // 2) % 4


def plan():
    steps = []

    def got(m, *chunks):
        steps.extend(("wait", m, q) for q in chunks)

    def spread(q):
        if q:
            got(0, q)
        steps.extend(("pass", m, 0, q) for m in (4, 1, 2))

    def pass5(*chunks):
        for q in chunks:
            got(4, q)
            steps.append(("pass", 5, 4, q))

    def pass3(*chunks):
        for q in chunks:
            got(1, q)
            got(2, q)
            steps.append(("pass", 3, 1 + q % 2, q))

    def names(m, *halves):
        steps.extend(("names", m, h) for h in halves)

    def product(i, rows, j, cols, sums):
        steps.append(("product", i, rows, j, cols, sums))

    whole, first, second = (0, BLK), (0, HALF), (HALF, HALF)
    steps.append(("pack", (2, 3, 1, 0)))
    steps.append(("meet",))
    steps.extend(("route", q) for q in (1, 2, 3))
    spread(0)
    steps.append(("pack", (6, 7, 4, 5)))
    steps.extend(("route", q) for q in (6, 7, 4, 5))
    spread(1)
    pass5(0)
    for q in (2, 3, 6, 7, 4, 5):
        spread(q)
    pass5(1, 2, 3)
    names(0, 0, 1)
    product(0, whole, 0, whole, "rows")
    pass3(0, 1, 2, 3)
    names(4, 0)
    names(1, 0)
    names(2, 0)
    product(0, whole, 4, first, "both")
    product(0, whole, 1, first, "both")
    pass5(6, 7)
    pass3(6, 7)
    pass5(4, 5)
    names(4, 1)
    product(0, whole, 4, second, "both")
    pass3(4, 5)
    names(1, 1)
    names(2, 1)
    product(2, whole, 4, whole, "both")
    product(1, whole, 4, whole, "both")
    product(0, whole, 1, second, "both")
    steps.append(("return", ((2, range(NQ)),)))
    got(5, 0, 1, 2, 3)
    names(5, 0)
    product(0, whole, 5, first, "rows")
    product(1, whole, 5, first, "both")
    got(3, 0, 1, 2, 3)
    names(3, 0)
    product(0, whole, 3, first, "rows")
    product(3, first, 4, whole, "both")
    product(3, first, 5, first, "rows")
    got(3, 6, 7, 4, 5)
    names(3, 1)
    product(0, whole, 3, second, "rows")
    product(3, second, 4, whole, "both")
    product(3, second, 5, first, "cols")
    steps.append(("return", ((3, range(NQ)), (4, range(NQ)), (5, range(4)))))
    got(5, 6, 7, 4, 5)
    names(5, 1)
    product(0, whole, 5, second, "rows")
    product(1, whole, 5, second, "both")
    product(3, whole, 5, second, "cols")
    steps.append(("return", ((5, range(4, NQ)), (1, range(NQ)), (0, range(NQ)))))
    return steps


def score_kernel(
    emb_ref,
    slot_ref,
    clu_ref,
    out_ref,
    flag_ref,
    held,
    unit,
    send,
    blk,
    lrow,
    lcol,
    rsum,
    csum,
    ret,
    got,
    emb_sem,
    arr_sem,
    out_sem,
    p1_out,
    ret_in,
    ret_out,
):
    gi = lax.axis_index("group")
    mi = lax.axis_index("member")
    x, c = gi // 2, gi % 2
    z, y = mi // 4, mi % 4

    def line_coord(t):
        return x * (1 - t) + z * t

    def line_dev(t, off, core):
        return (((x + (1 - t) * off) % 4) * 2 + core, ((z + t * off) % 4) * 4 + y)

    def plane_dev(a, b):
        px = (x + c * a) % 4
        pz = (z + (1 - c) * a) % 4
        py = (y + b * (1 + 2 * c)) % 4
        return (px * 2 + c, pz * 4 + py)

    def remote(src, dst, send_sem, recv_sem, dev):
        return pltpu.make_async_remote_copy(
            src_ref=src,
            dst_ref=dst,
            send_sem=send_sem,
            recv_sem=recv_sem,
            device_id=dev,
            device_id_type=MESH,
        )

    def chunk(m, q):
        return blk.at[m, pl.ds(q * CAPB, CAPB), :]

    barrier = pltpu.get_barrier_semaphore()
    partners = [(x * 2 + 1 - c, mi)]
    for off in (1, 2, 3):
        partners += [line_dev(c, off, c), line_dev(1 - c, off, 1 - c), line_dev(c, off, 1 - c)]
    partners += [plane_dev(1, 0), plane_dev(3, 0), plane_dev(0, 1), plane_dev(0, 3)]
    for dev in partners:
        pl.semaphore_signal(barrier, inc=1, device_id=dev, device_id_type=MESH)

    docs = emb_ref.shape[0]
    step_rows = docs // 4
    loads = []
    for k in range(4):
        rows = pl.ds(k * step_rows, step_rows)
        loads.append(pltpu.make_async_copy(emb_ref.at[rows], held.at[rows], emb_sem.at[k]))
        loads[k].start()

    group = slot_ref[...] // 128
    ids = lax.broadcasted_iota(jnp.int32, (8, docs), 0)
    member = (ids == group).astype(jnp.float32)
    upper = lax.broadcasted_iota(jnp.int32, (docs, docs), 0) < lax.broadcasted_iota(
        jnp.int32, (docs, docs), 1
    )
    before = jnp.dot(
        member.astype(jnp.bfloat16),
        upper.astype(jnp.float32).astype(jnp.bfloat16),
        preferred_element_type=jnp.float32,
    )
    rank = jnp.sum(member * before, axis=0, keepdims=True).astype(jnp.int32)
    fits = rank < DOCS
    place = jnp.where(fits, group * CAPB + rank, -1)

    lane = lax.broadcasted_iota(jnp.int32, (128, docs), 0)
    at_rank = ((lane == rank) & fits).astype(jnp.float32).astype(jnp.bfloat16)
    label = (member * (clu_ref[...] + 1).astype(jnp.float32)).astype(jnp.bfloat16)
    labels = lax.dot_general(
        label, at_rank, (((1,), (1,)), ((), ())), preferred_element_type=jnp.float32
    )
    tile_lane = lax.broadcasted_iota(jnp.int32, (8, 128), 1)
    tile_row = lax.broadcasted_iota(jnp.int32, (8, 128), 0)
    labels = jnp.where(tile_lane == FLAG_LANE, jnp.max(jnp.where(fits, 0.0, 1.0)), labels)

    rsum[...] = jnp.zeros_like(rsum)
    csum[...] = jnp.zeros_like(csum)
    for k in range(4):
        rows = pl.ds(k * step_rows, step_rows)
        loads[k].wait()
        values = held[rows, :]
        squares = jnp.sum(values * values, axis=1, keepdims=True)
        unit[rows, :] = (values * lax.rsqrt(squares + 1e-06)).astype(jnp.bfloat16)

    row = lax.broadcasted_iota(jnp.int32, (CAPB, docs), 0)
    last = lax.broadcasted_iota(jnp.int32, (CAPB, 128), 0) == DOCS

    def pack(chunks):
        owners = []
        for q in chunks:
            t, off = turn(c, q)
            owners.append(2 * ((line_coord(t) + off) % 4) + t)
        chosen = jnp.concatenate(
            [(row + g * CAPB == place).astype(jnp.float32) for g in owners], axis=0
        ).astype(jnp.bfloat16)
        packed = jnp.dot(chosen, unit[...], preferred_element_type=jnp.float32)
        for k, (q, g) in enumerate(zip(chunks, owners)):
            part = packed[k * CAPB : (k + 1) * CAPB]
            tail = jnp.sum(jnp.where(tile_row == g, labels, 0.0), axis=0, keepdims=True)
            part = jnp.concatenate([jnp.where(last, tail, part[:, :128]), part[:, 128:]], axis=1)
            if q:
                send[q] = part.astype(jnp.bfloat16)
            else:
                blk[0, 0:CAPB, :] = part.astype(jnp.bfloat16)

    sent = []

    def start(copy):
        copy.start()
        sent.append(copy)

    lanes = lax.broadcasted_iota(jnp.int32, (1, 128), 1)
    overflow = jnp.zeros((1, 128), jnp.float32)
    hops = {1: plane_dev(1, 0), 2: plane_dev(3, 0), 4: plane_dev(0, 1), 5: plane_dev(0, 1)}

    home = 2 * line_coord(c) + c

    def give_back(blocks, seen):
        flag = jnp.max(jnp.where(lanes == FLAG_LANE, seen, 0.0))
        for m, chunks in blocks:
            line = jnp.sum(csum[m], axis=0, keepdims=True)
            if m < 4:
                line = line + jnp.sum(jnp.transpose(rsum[m]), axis=0, keepdims=True)
            line = jnp.broadcast_to(line, (8, BLK))
            for q in chunks:
                piece = (pltpu.roll(line, BLK - q * CAPB, axis=1) if q else line)[0:1, 0:128]
                ret[m, q] = jnp.where(lanes == FLAG_LANE, flag, piece)
        for m, chunks in blocks:
            a, b = HELD[m]
            for q in chunks:
                if m == 0 and q == 0:
                    pltpu.make_async_copy(ret.at[0, 0], got.at[0, home], ret_in).start()
                    continue
                dl, cs = q // 2, q % 2
                core = c if cs == 0 else 1 - c
                px = (x + c * (4 - a) + (1 - c) * dl) % 4
                pz = (z + (1 - c) * (4 - a) + c * dl) % 4
                py = (y + (4 - b) * (1 + 2 * c)) % 4
                remote(
                    ret.at[m, q], got.at[m, home], ret_out, ret_in, (px * 2 + core, pz * 4 + py)
                ).start()

    for step in plan():
        if step[0] == "pack":
            pack(step[1])
        elif step[0] == "meet":
            pl.semaphore_wait(barrier, len(partners))
        elif step[0] == "return":
            give_back(step[1], overflow)
        elif step[0] == "route":
            q = step[1]
            t, off = turn(c, q)
            start(remote(send.at[q], chunk(0, q), p1_out.at[q], arr_sem.at[q], line_dev(t, off, t)))
        elif step[0] == "pass":
            _, m, src, q = step
            start(
                remote(
                    chunk(src, q), chunk(m, q), out_sem.at[(m - 1) * NQ + q],
                    arr_sem.at[m * NQ + q], hops[src if m == 3 else m],
                )
            )
        elif step[0] == "wait":
            _, m, q = step
            pltpu.make_async_copy(chunk(m, q), chunk(m, q), arr_sem.at[m * NQ + q]).wait()
        elif step[0] == "names":
            _, m, h = step
            rows = []
            for q in range(4 * h, 4 * h + 4):
                tail = blk[m, pl.ds(q * CAPB + CAPB - 16, 16), 0:128].astype(jnp.float32)
                rows.append(tail[15:16, :])
            found = jnp.concatenate(rows + [jnp.zeros((4, 128), jnp.float32)], axis=0)
            overflow = jnp.maximum(overflow, jnp.max(found, axis=0, keepdims=True))
            found = jnp.where(lanes < DOCS, found, 0.0)
            wide = jnp.zeros((8, HALF), jnp.float32)
            for k in range(4):
                piece = jnp.concatenate(
                    [
                        jnp.broadcast_to(found[k : k + 1, :], (8, 128)),
                        jnp.zeros((8, HALF - 128), jnp.float32),
                    ],
                    axis=1,
                )
                wide = wide + (pltpu.roll(piece, k * CAPB, axis=1) if k else piece)
            lrow[m, :, h * HALF : (h + 1) * HALF] = wide
            turned = jnp.transpose(
                jnp.concatenate([found, jnp.zeros((120, 128), jnp.float32)], axis=0)
            )
            for k in range(4):
                column = jnp.broadcast_to(turned[0:CAPB, k : k + 1], (CAPB, 128))
                lcol[m, pl.ds(h * HALF + k * CAPB, CAPB), :] = jnp.where(
                    column == 0.0, -1.0, column
                )
        else:
            _, i, (r0, nr), j, (c0, nc), sums = step
            tile = TILE if nr % TILE == 0 else nr
            for at in range(r0, r0 + nr, tile):
                cosine = lax.dot_general(
                    blk[i, pl.ds(at, tile), :],
                    blk[j, pl.ds(c0, nc), :],
                    (((1,), (1,)), ((), ())),
                    preferred_element_type=jnp.float32,
                )
                column = lcol[i, pl.ds(at, tile), :]
                total = jnp.zeros((tile, 128), jnp.float32)
                for n in range(nc // 128):
                    part = cosine[:, n * 128 : (n + 1) * 128]
                    here = slice(c0 + n * 128, c0 + (n + 1) * 128)
                    same = column == lrow[j, 0:1, here]
                    if i == j and at < here.stop and here.start < at + tile:
                        mine = at + lax.broadcasted_iota(jnp.int32, (tile, 128), 0)
                        other = here.start + lax.broadcasted_iota(jnp.int32, (tile, 128), 1)
                        same = same & (mine != other)
                    term = jnp.where(same, jnp.exp2(part * SCALE - SCALE), 0.0)
                    if sums != "cols":
                        total = total + term
                    if sums != "rows":
                        csum[j, :, here] += jnp.sum(term.reshape(tile // 8, 8, 128), axis=0)
                if sums != "cols":
                    rsum[i, pl.ds(at, tile), :] += total

    pltpu.make_async_copy(got, got, ret_in).wait()

    total = got[0, :, 0, :]
    for m in range(1, ND):
        total = total + got[m, :, 0, :]
    flag_ref[...] = jnp.max(jnp.where(tile_lane == FLAG_LANE, total, 0.0), keepdims=True)
    scores = jnp.log(1.0 + total)
    for n in range(docs // 128):
        here = slice(n * 128, (n + 1) * 128)
        spot = jnp.broadcast_to(jnp.minimum(rank[:, here], 127), (8, 128))
        picked = jnp.take_along_axis(scores, spot, axis=1)
        out_ref[:, here] = jnp.sum(
            jnp.where(tile_row == group[:, here], picked, 0.0), axis=0, keepdims=True
        )

    for copy in sent:
        copy.wait_send()
    most = ret.at[0, pl.ds(1, NQ - 1)]
    pltpu.make_async_copy(most, most, ret_out).wait()
    rest = ret.at[pl.ds(1, ND - 1)]
    pltpu.make_async_copy(rest, rest, ret_out).wait()


def fast(embeddings, cluster, slot):
    rows = embeddings.shape[0]
    dma = pltpu.SemaphoreType.DMA
    vmem = pl.BlockSpec(memory_space=pltpu.VMEM)
    return pl.pallas_call(
        score_kernel,
        out_shape=(
            jax.ShapeDtypeStruct((1, rows), jnp.float32),
            jax.ShapeDtypeStruct((1, 1), jnp.float32),
        ),
        in_specs=[pl.BlockSpec(memory_space=pl.ANY), vmem, vmem],
        out_specs=(vmem,) * 2,
        scratch_shapes=[
            pltpu.VMEM((rows, D), jnp.float32),
            pltpu.VMEM((rows, D), jnp.bfloat16),
            pltpu.VMEM((NQ, CAPB, D), jnp.bfloat16),
            pltpu.VMEM((ND, BLK, D), jnp.bfloat16),
            pltpu.VMEM((ND, 8, BLK), jnp.float32),
            pltpu.VMEM((ND, BLK, 128), jnp.float32),
            pltpu.VMEM((4, BLK, 128), jnp.float32),
            pltpu.VMEM((ND, 8, BLK), jnp.float32),
            pltpu.VMEM((ND, NQ, 1, 128), jnp.float32),
            pltpu.VMEM((ND, 8, 1, 128), jnp.float32),
            dma((4,)),
            dma((ND * NQ,)),
            dma(((ND - 1) * NQ,)),
            dma((NQ,)),
            dma(()),
            dma(()),
        ],
        compiler_params=pltpu.CompilerParams(
            collective_id=0, has_side_effects=True, vmem_limit_bytes=48 << 20
        ),
        name="scores",
    )(embeddings, slot.reshape(1, rows), cluster.reshape(1, rows))


def general(embeddings, cluster, slot):
    rows, width = embeddings.shape
    slots_dev = 2 * rows
    unit = (
        embeddings * lax.rsqrt(jnp.sum(embeddings * embeddings, axis=1, keepdims=True) + 1e-06)
    ).astype(jnp.bfloat16)
    both = ("group", "member")
    send_rows = jnp.zeros((slots_dev, width), jnp.bfloat16).at[slot].set(unit)
    send_labels = jnp.full((slots_dev,), -1, jnp.int32).at[slot].set(cluster)
    got_rows = lax.all_to_all(send_rows, both, split_axis=0, concat_axis=0, tiled=True)
    got_labels = lax.all_to_all(send_labels, both, split_axis=0, concat_axis=0, tiled=True)
    members = lax.axis_size("member")
    me = lax.axis_index("member")
    everyone = jnp.broadcast_to(got_rows[None], (members, slots_dev, width))
    keys = lax.all_to_all(everyone, "member", split_axis=0, concat_axis=0)
    names = jnp.broadcast_to(got_labels[None], (members, slots_dev))
    key_labels = lax.all_to_all(names, "member", split_axis=0, concat_axis=0)
    index = jnp.arange(slots_dev, dtype=jnp.int32)

    def step(k, totals):
        cosine = jnp.einsum("qd,kd->qk", got_rows, keys[k], preferred_element_type=jnp.float32)
        labels = key_labels[k]
        same = (got_labels[:, None] == labels[None, :]) & (labels[None, :] >= 0)
        same = same & (me * slots_dev + index[:, None] != k * slots_dev + index[None, :])
        terms = jnp.where(same, jnp.exp(20.0 * (cosine - 1.0)), jnp.float32(0.0))
        return totals + jnp.sum(terms, axis=1)

    totals = lax.fori_loop(0, members, step, jnp.zeros((slots_dev,), jnp.float32))
    scores = jnp.log(1.0 + totals)
    back = lax.all_to_all(scores, both, split_axis=0, concat_axis=0, tiled=True)
    return back[slot]


def body(embeddings, cluster, slot):
    out, flag = fast(embeddings, cluster, slot)
    return lax.cond(
        flag[0, 0] > 0.0,
        lambda: general(embeddings, cluster, slot),
        lambda: out.reshape(-1),
    )


def solution(mesh):
    spec = P(("group", "member"))
    in_specs = (P(("group", "member"), None), spec, spec)
    return jax.shard_map(body, mesh=mesh, in_specs=in_specs, out_specs=spec, check_vma=False)
```
